256 devices in a mesh: grp: 4 (over x), tp: 32 (over z, y), srv: 2 (over core).
Axes of the slice: x: 4, y: 4, z: 8, core: 2. Of those that a mesh axis runs over, the one named last changes fastest.
Arguments:
- tokens: bfloat16 [32768, 2048], P(('grp', 'tp', 'srv')), may hold values from -100 to 100
- norm_gain: float32 [2048], replicated, may hold values from 0.1 to 1.9
- query_weight: bfloat16 [2048, 4096], P(None, 'srv'), may hold values from -0.125 to 0.125
- key_matrix: bfloat16 [2048, 512], P(None, 'srv'), may hold values from -0.125 to 0.125
- value_matrix: bfloat16 [2048, 512], P(None, 'srv'), may hold values from -0.125 to 0.125
- query_gain: float32 [128], replicated, may hold values from 1.2 to 2.2
- key_gain: float32 [128], replicated, may hold values from 1.2 to 2.2
- lengths: int32 [32], replicated, may hold values from 1 to 4096, as said below
Outputs:
- attended: bfloat16 [32768, 4096], P(('grp', 'tp'), 'srv')
The draws below stay inside these ranges and needn't reach their ends.
Inputs may be any that keep to these rules, and one draw needn't show every extreme that they name: 32 document lengths in the order in which the documents are packed; they sum to 32768, the second to last of them is exactly 4096 and the last is 128.
All inputs are finite; a program needn't handle non-finite values.
Results may differ from the reference program's by a relative error of at most 0.012.
Values may be sent and summed in bfloat16 or wider, within the bound.
No kernel may reach another device: no remote copies, remote signals or barrier semaphores. Data moves between devices by JAX's collectives and lax.ppermute only.
A program may use at most 128 MiB of HBM per device.

```python
import math
import jax
import jax.numpy as jnp
from jax import lax

MODEL_WIDTH = 2048
QUERY_HEAD_COUNT = 32
KV_HEAD_COUNT = 4
HEAD_SIZE = 128
TOK_DEV = 256
DOC_MAX = 4096
PACKED_TOKENS = 32768
NDOC = 32


def draw_tokens(key, part):
    first_key = jax.random.fold_in(key, 11)
    normal_part = jnp.clip(jax.random.normal(first_key, (PACKED_TOKENS, MODEL_WIDTH), jnp.float32), -6.0, 6.0)
    result_array = normal_part.astype(jnp.bfloat16)
    return result_array


def draw_lengths(key, part):
    others = NDOC - 2
    closing = TOK_DEV // 2
    remaining = PACKED_TOKENS - DOC_MAX - closing
    baseline = remaining // others
    leftover = remaining - baseline * others
    counter = jnp.arange(others, dtype=jnp.int32)
    jitter = jax.random.randint(jax.random.fold_in(key, 21), (others,), 0, baseline // 2 + 1, dtype=jnp.int32)
    earlier = baseline + (counter < leftover).astype(jnp.int32) + jitter - jnp.roll(jitter, -1)
    return jnp.concatenate([earlier.astype(jnp.int32), jnp.full((1,), DOC_MAX, jnp.int32), jnp.full((1,), closing, jnp.int32)])


def block_scale(rng, extent, split, smallest, top_value):
    level, own = 1.0, jax.random.fold_in(rng, 6)
    for dim, blocks in split:
        heights = jnp.exp(jax.random.uniform(jax.random.fold_in(own, dim), (blocks,), jnp.float32, smallest / len(split), top_value / len(split)))
        level = level * jnp.repeat(heights, extent[dim] // blocks).reshape([-1 if axis == dim else 1 for axis in range(len(extent))])
    return level


def centred(stream_key, dims, spread, most, shards=(), kind=jnp.bfloat16):
    drawn = spread * jax.random.normal(stream_key, dims, jnp.float32)
    if shards:
        drawn = drawn * block_scale(stream_key, dims, shards, -0.22, 0.18)
    return jnp.clip(drawn, -most, most).astype(kind)


def setup_inputs(seed: int = 0) -> dict:
    streams_of = jax.random.split(jax.random.key(seed), 9)
    tokens = draw_tokens(jax.random.fold_in(streams_of[8], 71), 0)
    norm_gain = jnp.clip(1.0 + 0.18 * jax.random.normal(streams_of[1], (MODEL_WIDTH,), jnp.float32), 0.1, 1.9)
    query_weight = centred(streams_of[2], (MODEL_WIDTH, QUERY_HEAD_COUNT * HEAD_SIZE), MODEL_WIDTH ** -0.5, 0.125, ((1, 2),))
    key_matrix = centred(streams_of[3], (MODEL_WIDTH, KV_HEAD_COUNT * HEAD_SIZE), MODEL_WIDTH ** -0.5, 0.125, ((1, 2),))
    value_matrix = centred(streams_of[4], (MODEL_WIDTH, KV_HEAD_COUNT * HEAD_SIZE), MODEL_WIDTH ** -0.5, 0.125, ((1, 2),))
    query_gain = jnp.clip(jax.random.uniform(streams_of[5], (HEAD_SIZE,), jnp.float32, 1.2, 2.2), 1.2, 2.2)
    key_gain = jnp.clip(jax.random.uniform(streams_of[6], (HEAD_SIZE,), jnp.float32, 1.2, 2.2), 1.2, 2.2)
    lengths = draw_lengths(jax.random.fold_in(streams_of[8], 71), 0)
    return dict(tokens=tokens, norm_gain=norm_gain, query_weight=query_weight, key_matrix=key_matrix, value_matrix=value_matrix, query_gain=query_gain, key_gain=key_gain, lengths=lengths)


EPSILON = 1e-06
THETA = 1000000.0

def head_norm(value_rows, factor):
    scaled = value_rows * lax.rsqrt(lax.optimization_barrier(jnp.mean(value_rows * value_rows, axis=-1, keepdims=True)) + EPSILON)
    return scaled * factor

def rotate(value_rows, offsets):
    halfway = value_rows.shape[-1] // 2
    inverse = jnp.exp(-(2.0 * jnp.arange(halfway, dtype=jnp.float32) / value_rows.shape[-1]) * math.log(THETA))
    angles = offsets.astype(jnp.float32)[:, None] * inverse[None, :]
    cosine = jnp.cos(angles)[:, None, :]
    sinusoid = jnp.sin(angles)[:, None, :]
    former = value_rows[..., :halfway]
    latter = value_rows[..., halfway:]
    return jnp.concatenate([former * cosine - latter * sinusoid, latter * cosine + former * sinusoid], axis=-1)

def doc_bounds(positions, lengths):
    finish = jnp.cumsum(lengths).astype(jnp.int32)
    before = positions[:, None] >= finish[None, :]
    number = lax.optimization_barrier(jnp.sum(before.astype(jnp.int32), axis=1))
    opening = lax.optimization_barrier(jnp.max(jnp.where(before, finish[None, :], jnp.zeros_like(finish)[None, :]), axis=1))
    return (number, opening)

def reference(tokens, norm_gain, query_weight, key_matrix, value_matrix, query_gain, key_gain, lengths):
    positions = jnp.arange(PACKED_TOKENS, dtype=jnp.int32)
    unused_doc, opening = doc_bounds(positions, lengths)
    offsets = positions - opening
    floated = tokens.astype(jnp.float32)
    normalized_rows = (floated * lax.rsqrt(lax.optimization_barrier(jnp.mean(floated * floated, axis=-1, keepdims=True)) + EPSILON) * norm_gain).astype(jnp.bfloat16)
    query_raw = jnp.dot(normalized_rows, query_weight, preferred_element_type=jnp.float32).reshape(PACKED_TOKENS, QUERY_HEAD_COUNT, HEAD_SIZE)
    unnormed_keys = jnp.dot(normalized_rows, key_matrix, preferred_element_type=jnp.float32).reshape(PACKED_TOKENS, KV_HEAD_COUNT, HEAD_SIZE)
    value_rows = lax.optimization_barrier(jnp.dot(normalized_rows, value_matrix, preferred_element_type=jnp.float32).astype(jnp.bfloat16))
    value_rows = value_rows.reshape(PACKED_TOKENS, KV_HEAD_COUNT, HEAD_SIZE).astype(jnp.float32)
    query_rows = lax.optimization_barrier(rotate(head_norm(query_raw, query_gain), offsets).astype(jnp.bfloat16))
    query_rows = query_rows.reshape(PACKED_TOKENS, KV_HEAD_COUNT, QUERY_HEAD_COUNT // KV_HEAD_COUNT, HEAD_SIZE).astype(jnp.float32)
    key_rows = lax.optimization_barrier(rotate(head_norm(unnormed_keys, key_gain), offsets).astype(jnp.bfloat16))
    key_rows = key_rows.astype(jnp.float32)
    block_width = math.gcd(512, PACKED_TOKENS)
    scaling = HEAD_SIZE ** (-0.5)

    def one_block(block_number):
        begin_at = block_number * block_width
        query_block = lax.dynamic_slice_in_dim(query_rows, begin_at, block_width, 0)
        query_pos = begin_at + jnp.arange(block_width, dtype=jnp.int32)
        query_doc, query_open = doc_bounds(query_pos, lengths)
        lowest = query_open[0] // block_width

        def attend_block(key_number, running):
            accumulated, denominator = running
            key_start = key_number * block_width
            key_block = lax.dynamic_slice_in_dim(key_rows, key_start, block_width, 0)
            value_block = lax.dynamic_slice_in_dim(value_rows, key_start, block_width, 0)
            key_pos = key_start + jnp.arange(block_width, dtype=jnp.int32)
            key_doc, unused_open = doc_bounds(key_pos, lengths)
            allowed = (key_doc[None, :] == query_doc[:, None]) & (key_pos[None, :] <= query_pos[:, None])
            scores = jnp.einsum('qhgd,khd->qhgk', query_block, key_block) * scaling
            weights = jnp.where(allowed[:, None, None, :], jnp.exp(scores), 0.0)
            denominator = denominator + lax.optimization_barrier(jnp.sum(weights, axis=-1))
            rounded = lax.optimization_barrier(weights.astype(jnp.bfloat16)).astype(jnp.float32)
            accumulated = accumulated + jnp.einsum('qhgk,khd->qhgd', rounded, value_block)
            return (accumulated, denominator)
        starting_state = (jnp.zeros((block_width, KV_HEAD_COUNT, QUERY_HEAD_COUNT // KV_HEAD_COUNT, HEAD_SIZE), jnp.float32), jnp.zeros((block_width, KV_HEAD_COUNT, QUERY_HEAD_COUNT // KV_HEAD_COUNT), jnp.float32))
        accumulated, denominator = lax.fori_loop(lowest, block_number + 1, attend_block, starting_state)
        return (accumulated / denominator[..., None]).reshape(block_width, QUERY_HEAD_COUNT * HEAD_SIZE).astype(jnp.bfloat16)
    outputs = lax.map(one_block, jnp.arange(PACKED_TOKENS // block_width, dtype=jnp.int32))
    return outputs.reshape(PACKED_TOKENS, QUERY_HEAD_COUNT * HEAD_SIZE)
```

```python
import functools
import math

import jax
import jax.numpy as jnp
from jax import lax
from jax.experimental import pallas as pl
from jax.experimental.pallas import tpu as pltpu
from jax.sharding import PartitionSpec as P

EPSILON = 1e-06
THETA = 1000000.0
RING = 4
LEVELS = 5
AXES = ("grp", "tp")


VMEM = pltpu.VMEM
SMEM = pltpu.SMEM


def doc_bounds(positions, lengths):
    finish = jnp.cumsum(lengths)
    before = positions[:, None] >= finish[None, :]
    return jnp.max(jnp.where(before, finish[None, :], 0), axis=1)


def rope_tables(offsets, head_dim):
    halfway = head_dim // 2
    inverse = jnp.exp(
        -(2.0 * jnp.arange(halfway, dtype=jnp.float32) / head_dim) * math.log(THETA)
    )
    angles = offsets.astype(jnp.float32)[:, None] * inverse[None, :]
    cosine, sine = jnp.cos(angles), jnp.sin(angles)
    return (
        jnp.concatenate([cosine, cosine], axis=1),
        jnp.concatenate([-sine, sine], axis=1),
    )


def normed_and_rotated(head, gain, cosine, sine):
    scaled = head * lax.rsqrt(jnp.mean(head * head, axis=-1, keepdims=True) + EPSILON) * gain
    return scaled * cosine + pltpu.roll(scaled, scaled.shape[-1] // 2, 1) * sine


def kv_kernel(info, own, other, gain, wk, wv, key_gain, cosine, sine, kv, normed):
    half = own.shape[0]
    rows = 2 * half
    core = info[3]

    def put(ref, place):
        floated = ref[...].astype(jnp.float32)
        scale = lax.rsqrt(jnp.mean(floated * floated, axis=-1, keepdims=True) + EPSILON)
        normed[pl.ds(pl.multiple_of(place * half, half), half), :] = (
            floated * scale * gain[...]
        ).astype(jnp.bfloat16)

    put(own, core)
    put(other, 1 - core)
    raw = jnp.dot(normed[...], wk[...], preferred_element_type=jnp.float32)
    dim = key_gain.shape[1]
    for head in range(wk.shape[1] // dim):
        cols = slice(head * dim, (head + 1) * dim)
        kv[0:rows, cols] = normed_and_rotated(
            raw[:, cols], key_gain[...], cosine[...], sine[...]
        ).astype(jnp.bfloat16)
    kv[rows : 2 * rows, :] = jnp.dot(
        normed[...], wv[...], preferred_element_type=jnp.float32
    ).astype(jnp.bfloat16)


def query_kernel(factor, normed, wq, query_gain, cosine, sine, query):
    raw = jnp.dot(normed[...], wq[...], preferred_element_type=jnp.float32)
    dim = query_gain.shape[1]
    for head in range(wq.shape[1] // dim):
        cols = slice(head * dim, (head + 1) * dim)
        rotated = normed_and_rotated(raw[:, cols], query_gain[...], cosine[...], sine[...])
        query[head] = (rotated * factor).astype(jnp.bfloat16)


def attend_kernel(places, first, last, groups, info, query, opening, *refs):
    count = len(places)
    chunks = refs[:count]
    refs = refs[count:]
    if first:
        acc_in = den_in = None
    else:
        acc_in, den_in = refs[:2]
        refs = refs[2:]
    if last:
        out = refs[0]
        refs = refs[1:]
        acc, den, held, bias, sems = refs
    else:
        acc, den = refs[:2]
        held, bias, sems = refs[2:]
    heads, rows, dim = query.shape
    shard, lowest, highest_open = info[0], info[1], info[2]
    column = lax.rem(shard, RING)
    first_row = shard * rows
    reach = shard - lax.div(lowest, rows)
    bottom_level = min(k for k, _ in places)
    top_level = max(k for k, _ in places)
    low = jnp.maximum(RING * bottom_level + column - (RING - 1), 0)
    high = jnp.minimum(RING * top_level + column, reach)

    def distance(place):
        level, offset = place
        return RING * level + column - lax.rem(column + offset + RING, RING)

    def copy(index, slot):
        return pltpu.make_async_copy(chunks[index], held.at[slot], sems.at[slot])

    for index, place in enumerate(places):
        far = distance(place)

        @pl.when((far >= low) & (far <= high))
        def _():
            copy(index, far - low).start()

    for head in range(heads):
        acc[head] = jnp.zeros((rows, dim), jnp.float32) if first else acc_in[head]
        den[head] = jnp.zeros((rows, dim), jnp.float32) if first else den_in[head]

    def block(slot, masked):
        for head in range(heads):
            cols = pl.ds((head // groups) * dim, dim)
            scores = lax.dot_general(
                query[head],
                held[slot, 0:rows, cols],
                (((1,), (1,)), ((), ())),
                preferred_element_type=jnp.float32,
            )
            if masked:
                scores = scores + bias[...]
            weights = jnp.exp2(scores)
            parts = weights[:, 0:dim]
            for part in range(1, rows // dim):
                parts = parts + weights[:, part * dim : (part + 1) * dim]
            den[head] += parts
            acc[head] += jnp.dot(
                weights.astype(jnp.bfloat16),
                held[slot, rows : 2 * rows, cols],
                preferred_element_type=jnp.float32,
            )

    def step(far, carry):
        slot = far - low
        copy(0, slot).wait()
        start = (shard - far) * rows
        whole = (start >= highest_open) & (far > 0)

        @pl.when(whole)
        def _():
            block(slot, False)

        @pl.when(jnp.logical_not(whole))
        def _():
            key_at = start + lax.broadcasted_iota(jnp.int32, (rows, rows), 1)
            query_at = first_row + lax.broadcasted_iota(jnp.int32, (rows, rows), 0)
            allowed = (key_at >= opening[...]) & (key_at <= query_at)
            bias[...] = jnp.where(allowed, 0.0, -1e30)
            block(slot, True)

        return carry

    lax.fori_loop(low, high + 1, step, 0)
    if last:
        for head in range(heads):
            total = jnp.sum(den[head], axis=-1, keepdims=True)
            out[:, head * dim : (head + 1) * dim] = (acc[head] / total).astype(jnp.bfloat16)


def attend(places, chunks, info, query, opening, carried, last, groups):
    heads, rows, dim = query.shape
    first = carried is None
    state = jax.ShapeDtypeStruct((heads, rows, dim), jnp.float32)
    scratch = [
        VMEM((min(len(places), RING * LEVELS), 2 * rows, chunks[0].shape[1]), jnp.bfloat16),
        VMEM((rows, rows), jnp.float32),
        pltpu.SemaphoreType.DMA((len(places),)),
    ]
    whole = pl.BlockSpec(memory_space=VMEM)
    if last:
        out_shape = jax.ShapeDtypeStruct((rows, heads * dim), jnp.bfloat16)
        out_specs = whole
        scratch = [VMEM(state.shape, jnp.float32)] * 2 + scratch
    else:
        out_shape = (state, state)
        out_specs = (whole, whole)
    pairs = len(places) * heads * rows * rows
    return pl.pallas_call(
        functools.partial(attend_kernel, places, first, last, groups),
        out_shape=out_shape,
        in_specs=[pl.BlockSpec(memory_space=SMEM), whole, whole]
        + [pl.BlockSpec(memory_space=pl.ANY)] * len(places)
        + ([] if first else [whole, whole]),
        out_specs=out_specs,
        scratch_shapes=scratch,
        compiler_params=pltpu.CompilerParams(vmem_limit_bytes=40 * 1024 * 1024),
        cost_estimate=pl.CostEstimate(
            flops=4 * pairs * dim, bytes_accessed=8 << 20, transcendentals=pairs
        ),
        name="attend",
    )(info, query, opening, *chunks, *([] if first else carried))


def per_device(
    tokens, norm_gain, query_weight, key_matrix, value_matrix, query_gain, key_gain, lengths
):
    half, width = tokens.shape
    rows = 2 * half
    dim = query_gain.shape[0]
    pair = key_matrix.shape[1]
    heads = query_weight.shape[1] // dim
    groups = heads // (pair // dim)
    shards = lax.axis_size("grp") * lax.axis_size("tp")
    shard = lax.axis_index("grp") * lax.axis_size("tp") + lax.axis_index("tp")

    other = lax.ppermute(tokens, "srv", [(0, 1), (1, 0)])

    positions = shard * rows + jnp.arange(rows, dtype=jnp.int32)
    opening = doc_bounds(positions, lengths)
    cosine, sine = rope_tables(positions - opening, dim)
    info = jnp.stack([shard, opening[0], opening[-1], lax.axis_index("srv")]).astype(jnp.int32)
    opening = opening[:, None]

    whole = pl.BlockSpec(memory_space=VMEM)
    kv, normed = pl.pallas_call(
        kv_kernel,
        out_shape=(
            jax.ShapeDtypeStruct((2 * rows, pair), jnp.bfloat16),
            jax.ShapeDtypeStruct((rows, width), jnp.bfloat16),
        ),
        in_specs=[pl.BlockSpec(memory_space=SMEM)] + [whole] * 8,
        out_specs=(whole, whole),
        compiler_params=pltpu.CompilerParams(vmem_limit_bytes=40 * 1024 * 1024),
        name="keys_values",
    )(
        info,
        tokens,
        other,
        norm_gain[None, :],
        key_matrix,
        value_matrix,
        key_gain[None, :],
        cosine,
        sine,
    )

    tile = 256
    query = pl.pallas_call(
        functools.partial(query_kernel, dim**-0.5 * math.log2(math.e)),
        grid=(query_weight.shape[1] // tile,),
        out_shape=jax.ShapeDtypeStruct((heads, rows, dim), jnp.bfloat16),
        in_specs=[
            pl.BlockSpec((rows, width), lambda i: (0, 0)),
            pl.BlockSpec((width, tile), lambda i: (0, i)),
            pl.BlockSpec((1, dim), lambda i: (0, 0)),
            pl.BlockSpec((rows, dim), lambda i: (0, 0)),
            pl.BlockSpec((rows, dim), lambda i: (0, 0)),
        ],
        out_specs=pl.BlockSpec((tile // dim, rows, dim), lambda i: (i, 0, 0)),
        compiler_params=pltpu.CompilerParams(vmem_limit_bytes=40 * 1024 * 1024),
        cost_estimate=pl.CostEstimate(
            flops=2 * rows * width * heads * dim, bytes_accessed=11 << 20, transcendentals=0
        ),
        name="queries",
    )(normed, query_weight, query_gain[None, :], cosine, sine)

    def ring(step):
        return [
            (s, s - s % RING + (s + step) % RING) for s in range(shards)
        ]

    up = functools.partial(lax.ppermute, axis_name=AXES, perm=ring(1))
    down = functools.partial(lax.ppermute, axis_name=AXES, perm=ring(-1))
    ahead = functools.partial(
        lax.ppermute, axis_name=AXES, perm=[(s, (s + RING) % shards) for s in range(shards)]
    )

    held = {(0, 0): kv}
    for level in range(LEVELS):
        if level:
            held[level, 0] = ahead(held[level - 1, 0])
        held[level, -1] = up(held[level, 0])
        held[level, 1] = down(held[level, 0])
        if level == 0:
            held[level, 2] = up(held[level, -1])
        elif level == 1:
            held[level, 2] = down(held[level, 1])
        else:
            held[level, 2] = ahead(held[level - 1, 2])

    carried = None
    for levels in ((0, 1), (2,), (3, 4)):
        places = tuple(p for p in held if p[0] in levels)
        carried = attend(
            places,
            [held[p] for p in places],
            info,
            query,
            opening,
            carried,
            levels[-1] == LEVELS - 1,
            groups,
        )
    return carried


def solution(mesh):
    placed = (
        P(("grp", "tp", "srv"), None),
        P(),
        P(None, "srv"),
        P(None, "srv"),
        P(None, "srv"),
        P(),
        P(),
        P(),
    )
    return jax.shard_map(
        per_device, mesh=mesh, in_specs=placed, out_specs=P(AXES, "srv"), check_vma=False
    )
```

```python
import functools
import math

import jax
import jax.numpy as jnp
from jax import lax
from jax.experimental import pallas as pl
from jax.experimental.pallas import tpu as pltpu
from jax.sharding import PartitionSpec as P


EPSILON = 1e-06
THETA = 1000000.0
RING = 4
LEVELS = 5
AXES = ("grp", "tp")


VMEM = pltpu.VMEM
SMEM = pltpu.SMEM
WHOLE = pl.BlockSpec(memory_space=VMEM)
SCALARS = pl.BlockSpec(memory_space=SMEM)
PARAMS = pltpu.CompilerParams(vmem_limit_bytes=24 * 1024 * 1024)
STACK = 2


OPPOSITE = (
    lambda up, down, ahead: (up, 0, 2, (0, -1)),
    lambda up, down, ahead: (down, 1, 2, (1, 1)),
    lambda up, down, ahead: (up, 2, 2, (2, -1)),
    lambda up, down, ahead: (down, 3, 2, (3, 1)),
    lambda up, down, ahead: (up, 4, 2, (4, -1)),
)
USES = (
    ((0, 0), (0, -1), (0, 1)),
    ((0, 2), (1, 0), (1, -1), (1, 1)),
    ((1, 2), (2, 0), (2, -1), (2, 1)),
    ((2, 2), (3, 0), (3, -1), (3, 1)),
    ((3, 2), (4, 0), (4, -1), (4, 1)),
    ((4, 2),),
)


def normed_and_rotated(head, gain, cosine, sine):
    scaled = head * lax.rsqrt(jnp.mean(head * head, axis=-1, keepdims=True) + EPSILON) * gain
    return scaled * cosine + pltpu.roll(scaled, scaled.shape[-1] // 2, 1) * sine


def normed_rows(tokens, gain):
    floated = tokens.astype(jnp.float32)
    scale = lax.rsqrt(jnp.mean(floated * floated, axis=-1, keepdims=True) + EPSILON)
    return (floated * scale * gain).astype(jnp.bfloat16)


def keys_values(normed, wk, wv, key_gain, cosine, sine):
    raw = jnp.dot(normed, wk, preferred_element_type=jnp.float32)
    value = jnp.dot(normed, wv, preferred_element_type=jnp.float32).astype(jnp.bfloat16)
    dim = key_gain.shape[1]
    key = [
        normed_and_rotated(raw[:, at : at + dim], key_gain, cosine, sine).astype(jnp.bfloat16)
        for at in range(0, raw.shape[1], dim)
    ]
    return jnp.concatenate(key, axis=1), value


def half_at(core, half):
    return pl.ds(pl.multiple_of(core * half, half), half)


def table_kernel(lengths, info, opening, cosine, sine):
    rows, dim = cosine.shape
    shard = lax.axis_index("grp") * lax.axis_size("tp") + lax.axis_index("tp")
    first_row = shard * rows
    last_row = first_row + rows - 1

    def bounds(index, carry):
        finish, lowest, highest = carry
        finish = finish + lengths[index]
        return (
            finish,
            jnp.where(finish <= first_row, finish, lowest),
            jnp.where(finish <= last_row, finish, highest),
        )

    zero = jnp.int32(0)
    count = lengths.shape[0]
    _, lowest, highest = lax.fori_loop(0, count, bounds, (zero, zero, zero))
    info[0] = shard
    info[1] = lowest
    info[2] = highest
    position = first_row + lax.broadcasted_iota(jnp.int32, opening.shape, 0)
    opening[...] = jnp.full(opening.shape, lowest, jnp.int32)

    def mark(index, finish):
        finish = finish + lengths[index]

        @pl.when((finish > first_row) & (finish <= last_row))
        def _():
            opening[...] = jnp.where(position >= finish, finish, opening[...])

        return finish

    lax.fori_loop(0, count, mark, zero)
    halfway = dim // 2
    lane = lax.broadcasted_iota(jnp.int32, (1, dim), 1)
    index = jnp.where(lane < halfway, lane, lane - halfway).astype(jnp.float32)
    inverse = jnp.exp(-(2.0 * index / dim) * math.log(THETA))
    angles = (position - opening[...]).astype(jnp.float32) * inverse
    cosine[...] = jnp.cos(angles)
    sine[...] = jnp.where(lane < halfway, -1.0, 1.0) * jnp.sin(angles)


def key_value_kernel(own, other, gain, wk, wv, key_gain, cosine, sine, normed, kv):
    half = own.shape[0]
    rows = 2 * half
    core = lax.axis_index("srv")
    normed[half_at(core, half), :] = normed_rows(own[...], gain[...])
    normed[half_at(1 - core, half), :] = normed_rows(other[...], gain[...])
    key, value = keys_values(
        normed[...], wk[...], wv[...], key_gain[...], cosine[...], sine[...]
    )
    kv[0:rows, :] = key
    kv[rows : 2 * rows, :] = value


def query_kernel(factor, tile, normed, wq, query_gain, cosine, sine, query):
    rows, dim = cosine.shape
    steps = wq.shape[1] // tile

    def raw_of(step):
        return jnp.dot(
            normed[...], wq[:, step * tile : (step + 1) * tile], preferred_element_type=jnp.float32
        )

    raw = raw_of(0)
    for step in range(steps):
        later = raw_of(step + 1) if step + 1 < steps else None
        for part in range(tile // dim):
            head = step * (tile // dim) + part
            rotated = normed_and_rotated(
                raw[:, part * dim : (part + 1) * dim], query_gain[...], cosine[...], sine[...]
            )
            query[head * rows : (head + 1) * rows, :] = (rotated * factor).astype(jnp.bfloat16)
        raw = later


def attend_kernel(places, first, last, heads, info, query, opening, *refs):
    count = len(places)
    chunks = refs[:count]
    refs = refs[count if first else count + 2 :]
    acc, den = refs[:2]
    held, bias, fars, sems = refs[-4:]
    dim = query.shape[1]
    rows = query.shape[0] // heads
    shard, lowest, highest_open = info[0], info[1], info[2]
    column = lax.rem(shard, RING)
    first_row = shard * rows
    reach = shard - lax.div(lowest, rows)

    for index, (level, offset) in enumerate(places):
        far = RING * level + column - lax.rem(column + offset + RING, RING)
        wanted = (far >= 0) & (far <= reach)
        fars[index] = jnp.where(wanted, far, -1)

        @pl.when(wanted)
        def _():
            pltpu.make_async_copy(chunks[index], held.at[index], sems.at[index]).start()

    if first:
        acc[...] = jnp.zeros_like(acc)
        den[...] = jnp.zeros_like(den)

    stack = STACK * rows
    groups = heads * dim // chunks[0].shape[1]

    def scores_of(slot, part):
        cols = pl.ds((part * STACK // groups) * dim, dim)
        return lax.dot_general(
            query[part * stack : (part + 1) * stack, :],
            held[slot, 0:rows, cols],
            (((1,), (1,)), ((), ())),
            preferred_element_type=jnp.float32,
        )

    def block(slot):
        scores = scores_of(slot, 0)
        for part in range(heads // STACK):
            later = scores_of(slot, part + 1) if (part + 1) * STACK < heads else None
            cols = pl.ds((part * STACK // groups) * dim, dim)
            weights = jnp.exp2(scores + jnp.concatenate([bias[...]] * STACK, axis=0))
            lanes = weights[:, 0:dim]
            for at in range(dim, rows, dim):
                lanes = lanes + weights[:, at : at + dim]
            den[part * stack : (part + 1) * stack, :] += lanes
            acc[part * stack : (part + 1) * stack, :] += jnp.dot(
                weights.astype(jnp.bfloat16),
                held[slot, rows : 2 * rows, cols],
                preferred_element_type=jnp.float32,
            )
            scores = later

    def step(slot, carry):
        far = fars[slot]

        @pl.when(far >= 0)
        def _():
            pltpu.make_async_copy(chunks[0], held.at[slot], sems.at[slot]).wait()
            start = (shard - far) * rows
            whole = (start >= highest_open) & (far > 0)

            @pl.when(whole)
            def _():
                bias[...] = jnp.zeros_like(bias)

            @pl.when(jnp.logical_not(whole))
            def _():
                key_at = start + lax.broadcasted_iota(jnp.int32, (rows, rows), 1)
                query_at = first_row + lax.broadcasted_iota(jnp.int32, (rows, rows), 0)
                allowed = (key_at >= opening[:, 0:1]) & (key_at <= query_at)
                bias[...] = jnp.where(allowed, 0.0, -1e30)

            block(slot)

        return carry

    lax.fori_loop(0, count, step, 0)
    if last:
        out = refs[2]
        for head in range(heads):
            part = pl.ds(head * rows, rows)
            share = 1.0 / jnp.sum(den[part, :], axis=-1, keepdims=True)
            out[:, head * dim : (head + 1) * dim] = (acc[part, :] * share).astype(jnp.bfloat16)


def attend(places, chunks, info, query, opening, carried, last, heads):
    stacked, dim = query.shape
    rows = stacked // heads
    first = carried is None
    count = len(places)
    state = jax.ShapeDtypeStruct((stacked, dim), jnp.float32)
    out_shape = (state, state)
    if last:
        out_shape += (jax.ShapeDtypeStruct((rows, heads * dim), jnp.bfloat16),)
    pairs = count * stacked * rows
    return pl.pallas_call(
        functools.partial(attend_kernel, places, first, last, heads),
        out_shape=out_shape,
        in_specs=[SCALARS, WHOLE, WHOLE]
        + [pl.BlockSpec(memory_space=pl.ANY)] * count
        + ([] if first else [WHOLE, WHOLE]),
        out_specs=(WHOLE,) * len(out_shape),
        input_output_aliases={} if first else {3 + count: 0, 4 + count: 1},
        scratch_shapes=[
            VMEM((count, 2 * rows, chunks[0].shape[1]), jnp.bfloat16),
            VMEM((rows, rows), jnp.float32),
            SMEM((count,), jnp.int32),
            pltpu.SemaphoreType.DMA((count,)),
        ],
        compiler_params=PARAMS,
        cost_estimate=pl.CostEstimate(
            flops=4 * pairs * dim, bytes_accessed=8 << 20, transcendentals=pairs
        ),
        name="attend",
    )(info, query, opening, *chunks, *([] if first else carried))


def per_device(
    tokens, norm_gain, query_weight, key_matrix, value_matrix, query_gain, key_gain, lengths
):
    half, width = tokens.shape
    rows = 2 * half
    dim = query_gain.shape[0]
    pair = key_matrix.shape[1]
    heads = query_weight.shape[1] // dim
    shards = lax.axis_size("grp") * lax.axis_size("tp")

    other = lax.ppermute(tokens, "srv", [(0, 1), (1, 0)])
    gain, key_gain, query_gain = norm_gain[None, :], key_gain[None, :], query_gain[None, :]
    table = jax.ShapeDtypeStruct((rows, dim), jnp.float32)
    normed_shape = jax.ShapeDtypeStruct((rows, width), jnp.bfloat16)
    kv_shape = jax.ShapeDtypeStruct((2 * rows, pair), jnp.bfloat16)
    info, opening, cosine, sine = pl.pallas_call(
        table_kernel,
        out_shape=(
            jax.ShapeDtypeStruct((4,), jnp.int32),
            jax.ShapeDtypeStruct((rows, dim), jnp.int32),
            table,
            table,
        ),
        in_specs=[SCALARS],
        out_specs=(SCALARS,) + (WHOLE,) * 3,
        compiler_params=PARAMS,
        cost_estimate=pl.CostEstimate(flops=4 << 30, bytes_accessed=12 << 20, transcendentals=0),
        name="tables",
    )(lengths)
    normed, kv = pl.pallas_call(
        key_value_kernel,
        out_shape=(normed_shape, kv_shape),
        in_specs=[WHOLE] * 8,
        out_specs=(WHOLE, WHOLE),
        compiler_params=PARAMS,
        cost_estimate=pl.CostEstimate(flops=2 << 30, bytes_accessed=6 << 20, transcendentals=0),
        name="keys_values",
    )(tokens, other, gain, key_matrix, value_matrix, key_gain, cosine, sine)
    query_call = pl.pallas_call(
        functools.partial(query_kernel, dim**-0.5 * math.log2(math.e), 2 * dim),
        out_shape=jax.ShapeDtypeStruct((heads * rows, dim), jnp.bfloat16),
        in_specs=[WHOLE] * 5,
        out_specs=WHOLE,
        compiler_params=PARAMS,
        cost_estimate=pl.CostEstimate(
            flops=2 * rows * width * heads * dim, bytes_accessed=11 << 20, transcendentals=0
        ),
        name="queries",
    )
    query = query_call(normed, query_weight, query_gain, cosine, sine)

    def ring(step):
        return [
            (s, s - s % RING + (s + step) % RING) for s in range(shards)
        ]

    up = functools.partial(lax.ppermute, axis_name=AXES, perm=ring(1))
    down = functools.partial(lax.ppermute, axis_name=AXES, perm=ring(-1))
    ahead = functools.partial(
        lax.ppermute, axis_name=AXES, perm=[(s, (s + RING) % shards) for s in range(shards)]
    )

    held = {(0, 0): kv}

    def bring(move, level, offset, source):
        held[level, offset] = move(held[source])

    def use(places, carried, last=False):
        return attend(places, [held[p] for p in places], info, query, opening, carried, last, heads)

    def fetch(level):
        if level:
            bring(ahead, level, 0, (level - 1, 0))
        bring(up, level, -1, (level, 0))
        bring(down, level, 1, (level, 0))

    for level in range(LEVELS):
        fetch(level)
        bring(*OPPOSITE[level](up, down, ahead))
    carried = None
    for number, places in enumerate(USES):
        carried = use(places, carried, number == len(USES) - 1)
    return carried[2]


def solution(mesh):
    placed = (
        P(("grp", "tp", "srv"), None),
        P(),
        P(None, "srv"),
        P(None, "srv"),
        P(None, "srv"),
        P(),
        P(),
        P(),
    )
    return jax.shard_map(
        per_device, mesh=mesh, in_specs=placed, out_specs=P(AXES, "srv"), check_vma=False
    )
```

```python
import functools
import math

import jax
import jax.numpy as jnp
from jax import lax
from jax.experimental import pallas as pl
from jax.experimental.pallas import tpu as pltpu
from jax.sharding import PartitionSpec as P


EPSILON = 1e-06
THETA = 1000000.0
RING = 4
AXES = ("grp", "tp")


VMEM = pltpu.VMEM
SMEM = pltpu.SMEM
WHOLE = pl.BlockSpec(memory_space=VMEM)
SCALARS = pl.BlockSpec(memory_space=SMEM)
PARAMS = pltpu.CompilerParams(vmem_limit_bytes=24 * 1024 * 1024)
STACK = 2


MOVES = (
    (
        ("ahead", ((0, 0),), ((1, 0),)),
        ("up", ((0, 0),), ((0, -1),)),
        ("down", ((0, 0),), ((0, 1),)),
    ),
    (
        ("ahead", ((1, 0),), ((2, 0),)),
        ("down", ((1, 0),), ((1, 1),)),
        ("up", ((0, -1), (1, 0)), ((0, 2), (1, -1))),
    ),
    (
        ("ahead", ((2, 0),), ((3, 0),)),
        ("up", ((2, 0),), ((2, -1),)),
        ("down", ((1, 1), (2, 0)), ((1, 2), (2, 1))),
    ),
    (
        ("ahead", ((3, 0),), ((4, 0),)),
        ("down", ((3, 0),), ((3, 1),)),
        ("up", ((2, -1), (3, 0)), ((2, 2), (3, -1))),
    ),
    (
        ("up", ((4, 0),), ((4, -1),)),
        ("down", ((3, 1), (4, 0)), ((3, 2), (4, 1))),
    ),
    (("up", ((4, -1),), ((4, 2),)),),
)
USES = (
    ((0, 0),),
    ((0, -1), (0, 1), (1, 0)),
    ((0, 2), (1, -1), (1, 1), (2, 0)),
    ((1, 2), (2, -1), (2, 1), (3, 0)),
    ((2, 2), (3, -1), (3, 1), (4, 0)),
    ((3, 2), (4, -1), (4, 1)),
    ((4, 2),),
)


def normed_and_rotated(head, gain, cosine, sine):
    scaled = head * lax.rsqrt(jnp.mean(head * head, axis=-1, keepdims=True) + EPSILON) * gain
    return scaled * cosine + pltpu.roll(scaled, scaled.shape[-1] // 2, 1) * sine


def normed_rows(tokens, gain):
    floated = tokens.astype(jnp.float32)
    scale = lax.rsqrt(jnp.mean(floated * floated, axis=-1, keepdims=True) + EPSILON)
    return (floated * scale * gain).astype(jnp.bfloat16)


def keys_values(normed, wk, wv, key_gain, cosine, sine):
    raw = jnp.dot(normed, wk, preferred_element_type=jnp.float32)
    value = jnp.dot(normed, wv, preferred_element_type=jnp.float32).astype(jnp.bfloat16)
    dim = key_gain.shape[1]
    key = [
        normed_and_rotated(raw[:, at : at + dim], key_gain, cosine, sine).astype(jnp.bfloat16)
        for at in range(0, raw.shape[1], dim)
    ]
    return jnp.concatenate(key, axis=1), value


def half_at(core, half):
    return pl.ds(pl.multiple_of(core * half, half), half)


def table_kernel(lengths, info, opening, cosine, sine):
    rows, dim = cosine.shape
    shard = lax.axis_index("grp") * lax.axis_size("tp") + lax.axis_index("tp")
    first_row = shard * rows
    last_row = first_row + rows - 1

    def bounds(index, carry):
        finish, lowest, highest = carry
        finish = finish + lengths[index]
        return (
            finish,
            jnp.where(finish <= first_row, finish, lowest),
            jnp.where(finish <= last_row, finish, highest),
        )

    zero = jnp.int32(0)
    count = lengths.shape[0]
    _, lowest, highest = lax.fori_loop(0, count, bounds, (zero, zero, zero))
    info[0] = shard
    info[1] = lowest
    info[2] = highest
    position = first_row + lax.broadcasted_iota(jnp.int32, opening.shape, 0)
    opening[...] = jnp.full(opening.shape, lowest, jnp.int32)

    def mark(index, finish):
        finish = finish + lengths[index]

        @pl.when((finish > first_row) & (finish <= last_row))
        def _():
            opening[...] = jnp.where(position >= finish, finish, opening[...])

        return finish

    lax.fori_loop(0, count, mark, zero)
    halfway = dim // 2
    lane = lax.broadcasted_iota(jnp.int32, (1, dim), 1)
    index = jnp.where(lane < halfway, lane, lane - halfway).astype(jnp.float32)
    inverse = jnp.exp(-(2.0 * index / dim) * math.log(THETA))
    angles = (position - opening[...]).astype(jnp.float32) * inverse
    cosine[...] = jnp.cos(angles)
    sine[...] = jnp.where(lane < halfway, -1.0, 1.0) * jnp.sin(angles)


def key_value_kernel(own, other, gain, wk, wv, key_gain, cosine, sine, normed, kv):
    half = own.shape[0]
    rows = 2 * half
    core = lax.axis_index("srv")
    normed[half_at(core, half), :] = normed_rows(own[...], gain[...])
    normed[half_at(1 - core, half), :] = normed_rows(other[...], gain[...])
    key, value = keys_values(
        normed[...], wk[...], wv[...], key_gain[...], cosine[...], sine[...]
    )
    kv[0:rows, :] = key
    kv[rows : 2 * rows, :] = value


def query_kernel(factor, tile, normed, wq, query_gain, cosine, sine, query):
    rows, dim = cosine.shape
    steps = wq.shape[1] // tile

    def raw_of(step):
        return jnp.dot(
            normed[...], wq[:, step * tile : (step + 1) * tile], preferred_element_type=jnp.float32
        )

    raw = raw_of(0)
    for step in range(steps):
        later = raw_of(step + 1) if step + 1 < steps else None
        for part in range(tile // dim):
            head = step * (tile // dim) + part
            rotated = normed_and_rotated(
                raw[:, part * dim : (part + 1) * dim], query_gain[...], cosine[...], sine[...]
            )
            query[head * rows : (head + 1) * rows, :] = (rotated * factor).astype(jnp.bfloat16)
        raw = later


def attend_kernel(places, starts, first, last, heads, info, query, opening, *refs):
    count = len(places)
    chunks = refs[:count]
    refs = refs[count if first else count + 2 :]
    acc, den = refs[:2]
    held, bias, fars, sems = refs[-4:]
    dim = query.shape[1]
    rows = query.shape[0] // heads
    shard, lowest, highest_open = info[0], info[1], info[2]
    column = lax.rem(shard, RING)
    first_row = shard * rows
    reach = shard - lax.div(lowest, rows)

    for index, (level, offset) in enumerate(places):
        far = RING * level + column - lax.rem(column + offset + RING, RING)
        wanted = (far >= 0) & (far <= reach)
        fars[index] = jnp.where(wanted, far, -1)

        @pl.when(wanted)
        def _():
            block = chunks[index].at[pl.ds(starts[index], 2 * rows), :]
            pltpu.make_async_copy(block, held.at[index], sems.at[index]).start()

    if first:
        acc[...] = jnp.zeros_like(acc)
        den[...] = jnp.zeros_like(den)

    stack = STACK * rows
    groups = heads * dim // chunks[0].shape[1]

    def scores_of(slot, part):
        cols = pl.ds((part * STACK // groups) * dim, dim)
        return lax.dot_general(
            query[part * stack : (part + 1) * stack, :],
            held[slot, 0:rows, cols],
            (((1,), (1,)), ((), ())),
            preferred_element_type=jnp.float32,
        )

    def block(slot):
        scores = scores_of(slot, 0)
        for part in range(heads // STACK):
            later = scores_of(slot, part + 1) if (part + 1) * STACK < heads else None
            cols = pl.ds((part * STACK // groups) * dim, dim)
            weights = jnp.exp2(scores + jnp.concatenate([bias[...]] * STACK, axis=0))
            lanes = weights[:, 0:dim]
            for at in range(dim, rows, dim):
                lanes = lanes + weights[:, at : at + dim]
            den[part * stack : (part + 1) * stack, :] += lanes
            acc[part * stack : (part + 1) * stack, :] += jnp.dot(
                weights.astype(jnp.bfloat16),
                held[slot, rows : 2 * rows, cols],
                preferred_element_type=jnp.float32,
            )
            scores = later

    def step(slot, carry):
        far = fars[slot]

        @pl.when(far >= 0)
        def _():
            pltpu.make_async_copy(held.at[slot], held.at[slot], sems.at[slot]).wait()
            start = (shard - far) * rows
            whole = (start >= highest_open) & (far > 0)

            @pl.when(whole)
            def _():
                bias[...] = jnp.zeros_like(bias)

            @pl.when(jnp.logical_not(whole))
            def _():
                key_at = start + lax.broadcasted_iota(jnp.int32, (rows, rows), 1)
                query_at = first_row + lax.broadcasted_iota(jnp.int32, (rows, rows), 0)
                allowed = (key_at >= opening[:, 0:1]) & (key_at <= query_at)
                bias[...] = jnp.where(allowed, 0.0, -1e30)

            block(slot)

        return carry

    lax.fori_loop(0, count, step, 0)
    if last:
        out = refs[2]
        for head in range(heads):
            part = pl.ds(head * rows, rows)
            share = 1.0 / jnp.sum(den[part, :], axis=-1, keepdims=True)
            out[:, head * dim : (head + 1) * dim] = (acc[part, :] * share).astype(jnp.bfloat16)


def attend(places, blocks, size, info, query, opening, carried, last, heads):
    stacked, dim = query.shape
    rows = stacked // heads
    first = carried is None
    count = len(places)
    chunks = [chunk for chunk, _ in blocks]
    starts = [start for _, start in blocks]
    state = jax.ShapeDtypeStruct((stacked, dim), jnp.float32)
    out_shape = (state, state)
    if last:
        out_shape += (jax.ShapeDtypeStruct((rows, heads * dim), jnp.bfloat16),)
    pairs = count * stacked * rows
    return pl.pallas_call(
        functools.partial(attend_kernel, places, starts, first, last, heads),
        out_shape=out_shape,
        in_specs=[SCALARS, WHOLE, WHOLE]
        + [pl.BlockSpec(memory_space=pl.ANY)] * count
        + ([] if first else [WHOLE, WHOLE]),
        out_specs=(WHOLE,) * len(out_shape),
        input_output_aliases={} if first else {3 + count: 0, 4 + count: 1},
        scratch_shapes=[
            VMEM((count, size, chunks[0].shape[1]), jnp.bfloat16),
            VMEM((rows, rows), jnp.float32),
            SMEM((count,), jnp.int32),
            pltpu.SemaphoreType.DMA((count,)),
        ],
        compiler_params=PARAMS,
        cost_estimate=pl.CostEstimate(
            flops=4 * pairs * dim, bytes_accessed=8 << 20, transcendentals=pairs
        ),
        name="attend",
    )(info, query, opening, *chunks, *([] if first else carried))


def per_device(
    tokens, norm_gain, query_weight, key_matrix, value_matrix, query_gain, key_gain, lengths
):
    half, width = tokens.shape
    rows = 2 * half
    dim = query_gain.shape[0]
    pair = key_matrix.shape[1]
    heads = query_weight.shape[1] // dim
    shards = lax.axis_size("grp") * lax.axis_size("tp")

    other = lax.ppermute(tokens, "srv", [(0, 1), (1, 0)])
    gain, key_gain, query_gain = norm_gain[None, :], key_gain[None, :], query_gain[None, :]
    table = jax.ShapeDtypeStruct((rows, dim), jnp.float32)
    normed_shape = jax.ShapeDtypeStruct((rows, width), jnp.bfloat16)
    kv_shape = jax.ShapeDtypeStruct((2 * rows, pair), jnp.bfloat16)
    info, opening, cosine, sine = pl.pallas_call(
        table_kernel,
        out_shape=(
            jax.ShapeDtypeStruct((4,), jnp.int32),
            jax.ShapeDtypeStruct((rows, dim), jnp.int32),
            table,
            table,
        ),
        in_specs=[SCALARS],
        out_specs=(SCALARS,) + (WHOLE,) * 3,
        compiler_params=PARAMS,
        cost_estimate=pl.CostEstimate(flops=4 << 30, bytes_accessed=12 << 20, transcendentals=0),
        name="tables",
    )(lengths)
    normed, kv = pl.pallas_call(
        key_value_kernel,
        out_shape=(normed_shape, kv_shape),
        in_specs=[WHOLE] * 8,
        out_specs=(WHOLE, WHOLE),
        compiler_params=PARAMS,
        cost_estimate=pl.CostEstimate(flops=2 << 30, bytes_accessed=6 << 20, transcendentals=0),
        name="keys_values",
    )(tokens, other, gain, key_matrix, value_matrix, key_gain, cosine, sine)
    query_call = pl.pallas_call(
        functools.partial(query_kernel, dim**-0.5 * math.log2(math.e), 2 * dim),
        out_shape=jax.ShapeDtypeStruct((heads * rows, dim), jnp.bfloat16),
        in_specs=[WHOLE] * 5,
        out_specs=WHOLE,
        compiler_params=PARAMS,
        cost_estimate=pl.CostEstimate(
            flops=2 * rows * width * heads * dim, bytes_accessed=11 << 20, transcendentals=0
        ),
        name="queries",
    )
    query = query_call(normed, query_weight, query_gain, cosine, sine)

    def ring(step):
        return [
            (s, s - s % RING + (s + step) % RING) for s in range(shards)
        ]

    up = functools.partial(lax.ppermute, axis_name=AXES, perm=ring(1))
    down = functools.partial(lax.ppermute, axis_name=AXES, perm=ring(-1))
    ahead = functools.partial(
        lax.ppermute, axis_name=AXES, perm=[(s, (s + RING) % shards) for s in range(shards)]
    )

    ways = {"up": up, "down": down, "ahead": ahead}
    held = {(0, 0): (kv, 0)}
    size = kv.shape[0]
    for moves in MOVES:
        for way, sources, places in moves:
            blocks = [held[p][0] for p in sources]
            sent = blocks[0] if len(blocks) == 1 else jnp.concatenate(blocks, axis=0)
            came = ways[way](sent)
            for index, place in enumerate(places):
                held[place] = (came, index * size)

    def use(places, carried, last):
        blocks = [held[p] for p in places]
        return attend(places, blocks, size, info, query, opening, carried, last, heads)

    carried = None
    for number, places in enumerate(USES):
        carried = use(places, carried, number == len(USES) - 1)
    return carried[2]


def solution(mesh):
    placed = (
        P(("grp", "tp", "srv"), None),
        P(),
        P(None, "srv"),
        P(None, "srv"),
        P(None, "srv"),
        P(),
        P(),
        P(),
    )
    return jax.shard_map(
        per_device, mesh=mesh, in_specs=placed, out_specs=P(AXES, "srv"), check_vma=False
    )
```

```python
import functools
import math

import jax
import jax.numpy as jnp
from jax import lax
from jax.experimental import pallas as pl
from jax.experimental.pallas import tpu as pltpu
from jax.sharding import PartitionSpec as P


EPSILON = 1e-06
THETA = 1000000.0
RING = 4
AXES = ("grp", "tp")


VMEM = pltpu.VMEM
SMEM = pltpu.SMEM
WHOLE = pl.BlockSpec(memory_space=VMEM)
SCALARS = pl.BlockSpec(memory_space=SMEM)
PARAMS = pltpu.CompilerParams(vmem_limit_bytes=24 * 1024 * 1024)
STACK = 4


MOVES = (
    (
        ("ahead", ((0, 0),), ((1, 0),)),
        ("up", ((0, 0),), ((0, -1),)),
        ("down", ((0, 0),), ((0, 1),)),
    ),
    (
        ("ahead", ((1, 0),), ((2, 0),)),
        ("down", ((1, 0),), ((1, 1),)),
        ("up", ((0, -1), (1, 0)), ((0, 2), (1, -1))),
    ),
    (
        ("ahead", ((2, 0),), ((3, 0),)),
        ("up", ((2, 0),), ((2, -1),)),
        ("down", ((1, 1), (2, 0)), ((1, 2), (2, 1))),
    ),
    (
        ("ahead", ((3, 0),), ((4, 0),)),
        ("down", ((3, 0),), ((3, 1),)),
        ("up", ((2, -1), (3, 0)), ((2, 2), (3, -1))),
    ),
    (
        ("up", ((4, 0),), ((4, -1),)),
        ("down", ((4, 0),), ((4, 1),)),
        ("down", ((3, 1),), ((3, 2),)),
    ),
    (
        ("up", ((4, -1),), ((4, 2),)),
        ("down", ((4, 1),), ((4, 2),)),
    ),
)
USES = (
    ((0, 0),),
    ((0, -1), (0, 1), (1, 0)),
    ((0, 2), (1, -1), (1, 1), (2, 0)),
    ((1, 2), (2, -1), (2, 1), (3, 0)),
    ((2, 2), (3, -1), (3, 1), (4, 0)),
    ((3, 2), (4, -1), (4, 1)),
    ((4, 2),),
)


def normed_and_rotated(head, gain, cosine, sine):
    scaled = head * lax.rsqrt(jnp.mean(head * head, axis=-1, keepdims=True) + EPSILON) * gain
    return scaled * cosine + pltpu.roll(scaled, scaled.shape[-1] // 2, 1) * sine


def normed_rows(tokens, gain):
    floated = tokens.astype(jnp.float32)
    scale = lax.rsqrt(jnp.mean(floated * floated, axis=-1, keepdims=True) + EPSILON)
    return (floated * scale * gain).astype(jnp.bfloat16)


def keys_values(normed, wk, wv, key_gain, cosine, sine):
    raw = jnp.dot(normed, wk, preferred_element_type=jnp.float32)
    value = jnp.dot(normed, wv, preferred_element_type=jnp.float32).astype(jnp.bfloat16)
    dim = key_gain.shape[1]
    key = [
        normed_and_rotated(raw[:, at : at + dim], key_gain, cosine, sine).astype(jnp.bfloat16)
        for at in range(0, raw.shape[1], dim)
    ]
    return jnp.concatenate(key, axis=1), value


def half_at(core, half):
    return pl.ds(pl.multiple_of(core * half, half), half)


def table_kernel(lengths, info, opening, cosine, sine):
    rows, dim = cosine.shape
    shard = lax.axis_index("grp") * lax.axis_size("tp") + lax.axis_index("tp")
    first_row = shard * rows
    last_row = first_row + rows - 1

    def bounds(index, carry):
        finish, lowest, highest = carry
        finish = finish + lengths[index]
        return (
            finish,
            jnp.where(finish <= first_row, finish, lowest),
            jnp.where(finish <= last_row, finish, highest),
        )

    zero = jnp.int32(0)
    count = lengths.shape[0]
    _, lowest, highest = lax.fori_loop(0, count, bounds, (zero, zero, zero))
    info[0] = shard
    info[1] = lowest
    info[2] = highest
    position = first_row + lax.broadcasted_iota(jnp.int32, opening.shape, 0)
    opening[...] = jnp.full(opening.shape, lowest, jnp.int32)

    def mark(index, finish):
        finish = finish + lengths[index]

        @pl.when((finish > first_row) & (finish <= last_row))
        def _():
            opening[...] = jnp.where(position >= finish, finish, opening[...])

        return finish

    lax.fori_loop(0, count, mark, zero)
    halfway = dim // 2
    lane = lax.broadcasted_iota(jnp.int32, (1, dim), 1)
    index = jnp.where(lane < halfway, lane, lane - halfway).astype(jnp.float32)
    inverse = jnp.exp(-(2.0 * index / dim) * math.log(THETA))
    angles = (position - opening[...]).astype(jnp.float32) * inverse
    cosine[...] = jnp.cos(angles)
    sine[...] = jnp.where(lane < halfway, -1.0, 1.0) * jnp.sin(angles)


def key_value_kernel(own, other, gain, wk, wv, key_gain, cosine, sine, normed, kv):
    half = own.shape[0]
    rows = 2 * half
    core = lax.axis_index("srv")
    normed[half_at(core, half), :] = normed_rows(own[...], gain[...])
    normed[half_at(1 - core, half), :] = normed_rows(other[...], gain[...])
    key, value = keys_values(
        normed[...], wk[...], wv[...], key_gain[...], cosine[...], sine[...]
    )
    kv[0:rows, :] = key
    kv[rows : 2 * rows, :] = value


def query_kernel(factor, tile, normed, wq, query_gain, cosine, sine, query):
    rows, dim = cosine.shape
    steps = wq.shape[1] // tile

    def raw_of(step):
        return jnp.dot(
            normed[...], wq[:, step * tile : (step + 1) * tile], preferred_element_type=jnp.float32
        )

    raw = raw_of(0)
    for step in range(steps):
        later = raw_of(step + 1) if step + 1 < steps else None
        for part in range(tile // dim):
            head = step * (tile // dim) + part
            rotated = normed_and_rotated(
                raw[:, part * dim : (part + 1) * dim], query_gain[...], cosine[...], sine[...]
            )
            query[head * rows : (head + 1) * rows, :] = (rotated * factor).astype(jnp.bfloat16)
        raw = later


def attend_kernel(places, starts, first, last, heads, info, query, opening, *refs):
    count = len(places)
    arrays = sum(len(pieces) for pieces in starts)
    chunks = refs[:arrays]
    refs = refs[arrays if first else arrays + 2 :]
    acc, den = refs[:2]
    held, bias, fars, sems = refs[-4:]
    dim = query.shape[1]
    rows = query.shape[0] // heads
    shard, lowest, highest_open = info[0], info[1], info[2]
    column = lax.rem(shard, RING)
    first_row = shard * rows
    reach = shard - lax.div(lowest, rows)

    upcoming = iter(chunks)
    for index, (level, offset) in enumerate(places):
        sources = [next(upcoming) for _ in starts[index]]
        far = RING * level + column - lax.rem(column + offset + RING, RING)
        wanted = (far >= 0) & (far <= reach)
        fars[index] = jnp.where(wanted, far, -1)

        @pl.when(wanted)
        def _():
            to = 0
            for source, (start, part) in zip(sources, starts[index], strict=True):
                pltpu.make_async_copy(
                    source.at[pl.ds(start, part), :],
                    held.at[index, pl.ds(to, part), :],
                    sems.at[index],
                ).start()
                to += part

    if first:
        acc[...] = jnp.zeros_like(acc)
        den[...] = jnp.zeros_like(den)

    stack = STACK * rows
    groups = heads * dim // chunks[0].shape[1]

    def scores_of(slot, part):
        cols = pl.ds((part * STACK // groups) * dim, dim)
        return lax.dot_general(
            query[part * stack : (part + 1) * stack, :],
            held[slot, 0:rows, cols],
            (((1,), (1,)), ((), ())),
            preferred_element_type=jnp.float32,
        )

    def block(slot):
        scores = scores_of(slot, 0)
        for part in range(heads // STACK):
            later = scores_of(slot, part + 1) if (part + 1) * STACK < heads else None
            cols = pl.ds((part * STACK // groups) * dim, dim)
            weights = jnp.exp2(scores + jnp.concatenate([bias[...]] * STACK, axis=0))
            lanes = weights[:, 0:dim]
            for at in range(dim, rows, dim):
                lanes = lanes + weights[:, at : at + dim]
            den[part * stack : (part + 1) * stack, :] += lanes
            acc[part * stack : (part + 1) * stack, :] += jnp.dot(
                weights.astype(jnp.bfloat16),
                held[slot, rows : 2 * rows, cols],
                preferred_element_type=jnp.float32,
            )
            scores = later

    def step(slot, carry):
        far = fars[slot]

        @pl.when(far >= 0)
        def _():
            pltpu.make_async_copy(held.at[slot], held.at[slot], sems.at[slot]).wait()
            start = (shard - far) * rows
            whole = (start >= highest_open) & (far > 0)

            @pl.when(whole)
            def _():
                bias[...] = jnp.zeros_like(bias)

            @pl.when(jnp.logical_not(whole))
            def _():
                key_at = start + lax.broadcasted_iota(jnp.int32, (rows, rows), 1)
                query_at = first_row + lax.broadcasted_iota(jnp.int32, (rows, rows), 0)
                allowed = (key_at >= opening[:, 0:1]) & (key_at <= query_at)
                bias[...] = jnp.where(allowed, 0.0, -1e30)

            block(slot)

        return carry

    lax.fori_loop(0, count, step, 0)
    if last:
        out, ready, out_sems = refs[2:5]
        copies = []
        for head in range(heads):
            part = pl.ds(head * rows, rows)
            share = 1.0 / jnp.sum(den[part, :], axis=-1, keepdims=True)
            ready[:, head * dim : (head + 1) * dim] = (acc[part, :] * share).astype(jnp.bfloat16)
            if (head + 1) % 4 == 0:
                cols = (slice(None), slice((head - 3) * dim, (head + 1) * dim))
                copies.append(
                    pltpu.make_async_copy(ready.at[cols], out.at[cols], out_sems.at[head // 4])
                )
                copies[-1].start()
        for copy in copies:
            copy.wait()


def attend(places, blocks, size, info, query, opening, carried, last, heads):
    stacked, dim = query.shape
    rows = stacked // heads
    first = carried is None
    count = len(places)
    chunks = [array for pieces in blocks for array, _, _ in pieces]
    starts = [[(start, rows_of) for _, start, rows_of in pieces] for pieces in blocks]
    state = jax.ShapeDtypeStruct((stacked, dim), jnp.float32)
    out_shape = (state, state)
    if last:
        out_shape += (jax.ShapeDtypeStruct((rows, heads * dim), jnp.bfloat16),)
    pairs = count * stacked * rows
    return pl.pallas_call(
        functools.partial(attend_kernel, places, starts, first, last, heads),
        out_shape=out_shape,
        in_specs=[SCALARS, WHOLE, WHOLE]
        + [pl.BlockSpec(memory_space=pl.ANY)] * len(chunks)
        + ([] if first else [WHOLE, WHOLE]),
        out_specs=(WHOLE, WHOLE, pl.BlockSpec(memory_space=pl.ANY))[: len(out_shape)],
        input_output_aliases={} if first else {3 + len(chunks): 0, 4 + len(chunks): 1},
        scratch_shapes=(
            [VMEM((rows, heads * dim), jnp.bfloat16), pltpu.SemaphoreType.DMA((heads // 4,))]
            if last
            else []
        )
        + [
            VMEM((count, size, chunks[0].shape[1]), jnp.bfloat16),
            VMEM((rows, rows), jnp.float32),
            SMEM((count,), jnp.int32),
            pltpu.SemaphoreType.DMA((count,)),
        ],
        compiler_params=PARAMS,
        cost_estimate=pl.CostEstimate(
            flops=4 * pairs * dim, bytes_accessed=8 << 20, transcendentals=pairs
        ),
        name="attend",
    )(info, query, opening, *chunks, *([] if first else carried))


def per_device(
    tokens, norm_gain, query_weight, key_matrix, value_matrix, query_gain, key_gain, lengths
):
    half, width = tokens.shape
    rows = 2 * half
    dim = query_gain.shape[0]
    pair = key_matrix.shape[1]
    heads = query_weight.shape[1] // dim
    shards = lax.axis_size("grp") * lax.axis_size("tp")

    other = lax.ppermute(tokens, "srv", [(0, 1), (1, 0)])
    gain, key_gain, query_gain = norm_gain[None, :], key_gain[None, :], query_gain[None, :]
    table = jax.ShapeDtypeStruct((rows, dim), jnp.float32)
    normed_shape = jax.ShapeDtypeStruct((rows, width), jnp.bfloat16)
    kv_shape = jax.ShapeDtypeStruct((2 * rows, pair), jnp.bfloat16)
    info, opening, cosine, sine = pl.pallas_call(
        table_kernel,
        out_shape=(
            jax.ShapeDtypeStruct((4,), jnp.int32),
            jax.ShapeDtypeStruct((rows, dim), jnp.int32),
            table,
            table,
        ),
        in_specs=[SCALARS],
        out_specs=(SCALARS,) + (WHOLE,) * 3,
        compiler_params=PARAMS,
        cost_estimate=pl.CostEstimate(flops=4 << 30, bytes_accessed=12 << 20, transcendentals=0),
        name="tables",
    )(lengths)
    normed, kv = pl.pallas_call(
        key_value_kernel,
        out_shape=(normed_shape, kv_shape),
        in_specs=[WHOLE] * 8,
        out_specs=(WHOLE, WHOLE),
        compiler_params=PARAMS,
        cost_estimate=pl.CostEstimate(flops=2 << 30, bytes_accessed=6 << 20, transcendentals=0),
        name="keys_values",
    )(tokens, other, gain, key_matrix, value_matrix, key_gain, cosine, sine)
    query_call = pl.pallas_call(
        functools.partial(query_kernel, dim**-0.5 * math.log2(math.e), 2 * dim),
        out_shape=jax.ShapeDtypeStruct((heads * rows, dim), jnp.bfloat16),
        in_specs=[WHOLE] * 5,
        out_specs=WHOLE,
        compiler_params=PARAMS,
        cost_estimate=pl.CostEstimate(
            flops=2 * rows * width * heads * dim, bytes_accessed=11 << 20, transcendentals=0
        ),
        name="queries",
    )
    query = query_call(normed, query_weight, query_gain, cosine, sine)

    def ring(step):
        return [
            (s, s - s % RING + (s + step) % RING) for s in range(shards)
        ]

    up = functools.partial(lax.ppermute, axis_name=AXES, perm=ring(1))
    down = functools.partial(lax.ppermute, axis_name=AXES, perm=ring(-1))
    ahead = functools.partial(
        lax.ppermute, axis_name=AXES, perm=[(s, (s + RING) % shards) for s in range(shards)]
    )

    ways = {"up": up, "down": down, "ahead": ahead}
    size = kv.shape[0]
    held = {(0, 0): [(kv, 0, size)]}
    for moves in MOVES:
        targets = [place for _, _, places in moves for place in places]
        for way, sources, places in moves:
            shared = targets.count(places[0])
            rows_of = size // shared
            blocks = [held[p][0][0] for p in sources]
            if shared > 1:
                at = rows_of * len(held.get(places[0], ()))
                blocks = [block[at : at + rows_of] for block in blocks]
            sent = blocks[0] if len(blocks) == 1 else jnp.concatenate(blocks, axis=0)
            came = ways[way](sent)
            for index, place in enumerate(places):
                held.setdefault(place, []).append((came, index * rows_of, rows_of))

    def use(places, carried, last):
        blocks = [held[p] for p in places]
        return attend(places, blocks, size, info, query, opening, carried, last, heads)

    carried = None
    for number, places in enumerate(USES):
        carried = use(places, carried, number == len(USES) - 1)
    return carried[2]


def solution(mesh):
    placed = (
        P(("grp", "tp", "srv"), None),
        P(),
        P(None, "srv"),
        P(None, "srv"),
        P(None, "srv"),
        P(),
        P(),
        P(),
    )
    return jax.shard_map(
        per_device, mesh=mesh, in_specs=placed, out_specs=P(AXES, "srv"), check_vma=False
    )
```
